32 devices in a mesh: wide: 16 (over z, y, core), blk: 2 (over x).
Axes of the slice: x: 2, y: 2, z: 4, core: 2. Of those that a mesh axis runs over, the one named last changes fastest.
Arguments:
- position: float32 [3, 4096], P(None, ('wide', 'blk')), may hold values from -1 to 1, as said below
- order_field: float32 [12, 4096], P(None, ('wide', 'blk')), may hold values from -1.5 to 1.5
- cell_area: float32 [4096], P(('wide', 'blk')), may hold values from 0.5 to 2
- slot_vertex: int32 [16, 2, 16, 24], P('wide', 'blk'), may hold values from 0 to 127
- send_count: int32 [16, 2, 16], P('wide', 'blk'), may hold values from 0 to 24, as said below
- corner_slot: int32 [16, 2, 3, 256], P('wide', 'blk'), may hold values from 0 to 383, as said below
- edge_weight: float32 [16, 2, 3, 256], P('wide', 'blk'), may hold values from 0.2 to 2
Outputs:
- potential: float32 [12, 4096], P(None, ('wide', 'blk'))
The draws below stay inside these ranges and needn't reach their ends.
Inputs may be any that keep to these rules, and one draw needn't show every extreme that they name: `position`: each column is a unit vector. `slot_vertex`: slots of a block at or beyond the matching send_count are padding and hold arbitrary numbers. send_count[p, b, q] is how many leading slots of block [p, b, q] are live. It is nonzero exactly when (q - p) mod 16 is one of 0, 1, 2, 8, 15, 14, and then at least 12; every owner keeps all 24 slots live for one of the five requesters with (q - p) mod 16 among 0, 1, 2, 15, 14. `corner_slot`: A value c of requester (q, b) names slot c % 24 of owner (c // 24, b); it is always a live slot, and every live slot is named by some corner.
All inputs are finite; a program needn't handle non-finite values.
Results may differ from the reference program's by a relative error of at most 0.0003.
Values sent between devices are 32-bit elements; how exact they have to be, the bound alone decides.
A program may use at most 64 MiB of HBM per device.

```python
import functools
import math
import jax
import jax.numpy as jnp
from jax import lax

V_DEV = 128
SLOTS = 24
ELEM_DEV = 256
FIELDS = 12
VERTS = 4096
N_WIDE = 16
N_BLK = 2


def sphere_points(key):
    raw_normal = jax.random.normal(jax.random.fold_in(key, 101), (3, VERTS), jnp.float32)
    length = jnp.sqrt(jnp.sum(raw_normal * raw_normal, axis=0, keepdims=True) + 1e-12)
    return raw_normal / length


def pair_counts(key):
    lowest = max(1, SLOTS // 2)
    base_count = jax.random.randint(jax.random.fold_in(key, 303), (N_WIDE, N_BLK, N_WIDE), lowest, SLOTS + 1)
    owner_ids = jnp.arange(N_WIDE, dtype=jnp.int32)
    offset_map = (owner_ids[None, None, :] - owner_ids[:, None, None]) % N_WIDE
    nearby = (offset_map <= 2) | (offset_map >= N_WIDE - 2) | (offset_map == N_WIDE // 2)
    full_pick = jax.random.randint(jax.random.fold_in(key, 304), (N_WIDE, N_BLK), -2, 3)
    full_rank = (owner_ids[:, None] + full_pick) % N_WIDE
    forced = owner_ids[None, None, :] == full_rank[:, :, None]
    return jnp.where(forced, SLOTS, jnp.where(nearby, base_count, 0)).astype(jnp.int32)


def draw_position(key, part):
    return sphere_points(key)


def draw_order_field(key, part):
    ramp_line = 0.3 + 0.6 * jnp.arange(VERTS, dtype=jnp.float32) / VERTS
    noise_key = jax.random.fold_in(key, 202)
    rough = 0.4 * jax.random.normal(noise_key, (FIELDS, VERTS), jnp.float32)
    values = ramp_line[None, :] + rough
    return jnp.clip(values, -1.5, 1.5)


def draw_send_count(key, part):
    return pair_counts(key)


def draw_corner_slot(key, part):
    counts = pair_counts(key)
    needed = jnp.transpose(counts, (2, 1, 0))
    flat_slot = jnp.arange(N_WIDE * SLOTS, dtype=jnp.int32)
    live_int = ((flat_slot % SLOTS)[None, None, :] < jnp.repeat(needed, SLOTS, axis=2)).astype(jnp.int32)
    live_total = jnp.sum(live_int, axis=2)
    ordering = jnp.argsort(1 - live_int, axis=2, stable=True).astype(jnp.int32)
    key_list = jax.random.split(jax.random.fold_in(key, 405), N_WIDE * N_BLK)
    shuffles = jax.vmap(lambda one_key: jax.random.permutation(one_key, 3 * ELEM_DEV))(key_list)
    shuffles = shuffles.reshape(N_WIDE, N_BLK, 3 * ELEM_DEV).astype(jnp.int32)
    choose = shuffles % live_total[:, :, None]
    chosen = jnp.take_along_axis(ordering, choose, axis=2)
    return chosen.reshape(N_WIDE, N_BLK, 3, ELEM_DEV).astype(jnp.int32)


def touch_ends(entries, stream_key, smallest, top_value):
    longest = entries.shape.index(max(entries.shape))
    spots = []
    for shift in (0, 1):
        where = [jax.random.randint(jax.random.fold_in(stream_key, axis), (), 0, length) for axis, length in enumerate(entries.shape)]
        where[longest] = (where[longest] + shift) % entries.shape[longest]
        spots.append(tuple(where))
    return entries.at[spots[0]].set(smallest).at[spots[1]].set(top_value)


def block_scale(own_key, shape, cuts, least, top_value):
    def one(dim, blocks):
        heights = jax.random.uniform(jax.random.fold_in(jax.random.fold_in(own_key, 6), dim), (blocks,), jnp.float32, least / len(cuts), top_value / len(cuts))
        return jnp.repeat(jnp.exp(heights), shape[dim] // blocks).reshape((-1,) + (1,) * (len(shape) - dim - 1))

    factor_of = one(*cuts[0])
    for cut in cuts[1:]:
        factor_of = factor_of * one(*cut)
    return factor_of


def setup_inputs(seed: int = 0) -> dict:
    splits = jax.random.split(jax.random.key(seed), 8)
    return {
        "position": draw_position(jax.random.fold_in(splits[7], 71), 0),
        "order_field": draw_order_field(jax.random.fold_in(splits[7], 71), 0),
        "cell_area": jnp.clip(jnp.exp(math.log(2.0) - 1.3862944 * jax.random.uniform(splits[2], (VERTS,), jnp.float32) ** block_scale(splits[2], (VERTS,), ((0, 32),), -0.2, 0.2)), 0.5, 2.0),
        "slot_vertex": touch_ends(jax.random.randint(splits[3], (N_WIDE, N_BLK, N_WIDE, SLOTS), 0, V_DEV), jax.random.fold_in(splits[3], 1), 0, V_DEV - 1).astype(jnp.int32),
        "send_count": draw_send_count(jax.random.fold_in(splits[7], 71), 0),
        "corner_slot": draw_corner_slot(jax.random.fold_in(splits[7], 71), 0),
        "edge_weight": jnp.clip(jnp.exp(math.log(2.0) - 2.3025851 * jax.random.uniform(splits[6], (N_WIDE, N_BLK, 3, ELEM_DEV), jnp.float32) ** block_scale(splits[6], (N_WIDE, N_BLK, 3, ELEM_DEV), ((0, 16), (1, 2)), -0.2, 0.2)), 0.2, 2.0),
    }


stiff_coef = 0.1
source_block = 2048


def kernel_sum(targets, sources, weights, soften):
    number = sources.shape[1]
    block_len = math.gcd(number, source_block)

    def add_block(block_id, running):
        first_col = block_id * block_len
        source_pos = lax.dynamic_slice_in_dim(sources, first_col, block_len, 1)
        source_mass = lax.dynamic_slice_in_dim(weights, first_col, block_len, 1)
        distance = (targets[0][:, None] - source_pos[0][None, :]) ** 2
        distance = distance + (targets[1][:, None] - source_pos[1][None, :]) ** 2
        distance = distance + (targets[2][:, None] - source_pos[2][None, :]) ** 2
        kernel = jnp.log(distance + soften)
        return running + jnp.einsum("fs,ts->ft", source_mass, kernel, precision=lax.Precision.HIGHEST)

    start_sum = jnp.zeros((weights.shape[0], targets.shape[1]), jnp.float32)
    return lax.fori_loop(0, number // block_len, add_block, start_sum)


def corner_terms(values, weights):
    value_a, value_b, value_c = values[..., 0, :], values[..., 1, :], values[..., 2, :]
    weight_a, weight_b, weight_c = weights[..., 0, :], weights[..., 1, :], weights[..., 2, :]
    term_a = weight_c * (value_a - value_b) + weight_b * (value_a - value_c)
    term_b = weight_c * (value_b - value_a) + weight_a * (value_b - value_c)
    term_c = weight_b * (value_c - value_a) + weight_a * (value_c - value_b)
    return jnp.stack([term_a, term_b, term_c], axis=-2)


def reference(position, order_field, cell_area, slot_vertex, send_count, corner_slot, edge_weight):
    vertex_total = position.shape[1]
    fields = order_field.shape[0]
    average = jnp.sum(cell_area[None, :] * order_field, axis=1) / jnp.sum(cell_area)
    masses = cell_area[None, :] * (order_field - average[:, None])
    soften = 4.0 / vertex_total
    block_len = math.gcd(vertex_total, 128)
    tiles = position.reshape(3, vertex_total // block_len, block_len).transpose(1, 0, 2)
    runner = functools.partial(kernel_sum, sources=position, weights=masses, soften=soften)
    pieces = lax.map(runner, tiles)
    summed = pieces.transpose(1, 0, 2).reshape(fields, vertex_total)
    long_range = -(vertex_total ** -0.5) * summed

    wide_count = slot_vertex.shape[0]
    blk_count = slot_vertex.shape[1]
    slot_len = slot_vertex.shape[3]
    per_device = vertex_total // (wide_count * blk_count)
    owner_id = (corner_slot // slot_len).astype(jnp.int32)
    within = (corner_slot % slot_len).astype(jnp.int32)
    requester = jnp.arange(wide_count, dtype=jnp.int32)[:, None, None, None]
    column = jnp.arange(blk_count, dtype=jnp.int32)[None, :, None, None]
    local_id = slot_vertex[owner_id, column, requester, within]
    live_slot = within < send_count[owner_id, column, requester]
    global_id = ((owner_id * blk_count + column) * per_device + local_id).astype(jnp.int32)
    values = jnp.where(live_slot[None], order_field[:, global_id], 0.0)
    corner_sum = jnp.where(live_slot[None], corner_terms(values, edge_weight), 0.0)
    stiffness = jnp.zeros((fields, vertex_total), jnp.float32).at[:, global_id.reshape(-1)].add(
        corner_sum.reshape(fields, -1))
    return order_field ** 3 - order_field + stiff_coef * stiffness / cell_area[None, :] + long_range
```

```python
import functools

import jax
import jax.numpy as jnp
from jax import lax
from jax.experimental import pallas as pl
from jax.experimental.pallas import tpu as pltpu
from jax.sharding import PartitionSpec as P

stiff_coef = 0.1
LANES = 128
GROUP = 4
MESH = pl.DeviceIdType.MESH
NT = (((1,), (1,)), ((), ()))
NN = (((1,), (0,)), ((), ()))


def halves(x):
    hi = x.astype(jnp.bfloat16)
    lo = (x - hi.astype(jnp.float32)).astype(jnp.bfloat16)
    return hi, lo


def stacked(x):
    return jnp.concatenate(halves(x), axis=0)


def mm(a, b, dims):
    return lax.dot_general(a, b, dims, preferred_element_type=jnp.float32)


def kernel(
    wide, blk, fields, slot_len,
    pos_ref, order_ref, area_ref, slot_ref, count_ref, corner_ref, weight_ref,
    out_ref,
    blocks, vout, vbuf, rout, rbuf, targets, acc_ref, sum_ref,
    bsend, brecv, vsend, vrecv, rsend, rrecv,
):
    n = wide * blk
    my_w, my_b = lax.axis_index("wide"), lax.axis_index("blk")
    me = my_w * blk + my_b
    rows = fields + 4
    soften = 4.0 / (n * LANES)
    strength = float(n * LANES) ** (-0.5)
    offsets = (1, wide - 1, 2, wide - 2, wide // 2)

    def device(step):
        to = lax.rem(me + step, n)
        return (to // blk, lax.rem(to, blk))

    barrier = pltpu.get_barrier_semaphore()

    def greet(step, carry):
        pl.semaphore_signal(barrier, inc=1, device_id=device(step), device_id_type=MESH)
        return carry

    lax.fori_loop(1, n, greet, 0)

    blocks[0, :fields] = order_ref[...]
    blocks[0, fields:fields + 3] = pos_ref[...]
    blocks[0, fields + 3:] = area_ref[...]
    own = jnp.concatenate([order_ref[...], pos_ref[...], area_ref[...]], axis=0)
    area = area_ref[...]

    lane = lax.broadcasted_iota(jnp.int32, (1, 2 * LANES), 1)
    base = jnp.full((1, 2 * LANES), -1, jnp.int32)
    towards = jnp.full((1, 2 * LANES), -1, jnp.int32)
    for k, offset in enumerate(offsets + (0,)):
        first = k * slot_len if offset else LANES
        inside = (lane >= first) & (lane < first + slot_len)
        base = jnp.where(inside, lane - first, base)
        towards = jnp.where(inside, lax.rem(my_w + offset, wide), towards)
    count_lane = lax.broadcasted_iota(jnp.int32, (wide, wide), 1)
    count_row = lax.broadcasted_iota(jnp.int32, (wide, wide), 0)
    counts = count_ref[0].astype(jnp.float32)
    counts = jnp.sum(jnp.where(count_lane == count_row, counts, 0.0), axis=1, keepdims=True)
    slot_id = lax.broadcasted_iota(jnp.int32, (wide, slot_len), 1).astype(jnp.float32)
    table = jnp.where(slot_id < counts, slot_ref[0, 0].astype(jnp.float32) + 1.0, 0.0)
    spread_row = lax.broadcasted_iota(jnp.int32, (slot_len, 2 * LANES), 0)
    spread = jnp.where(spread_row == base, 1.0, 0.0).astype(jnp.bfloat16)
    spread_table = mm(table.astype(jnp.bfloat16), spread, NN)
    wide_row = lax.broadcasted_iota(jnp.int32, (wide, 2 * LANES), 0)
    vertex_of = jnp.sum(jnp.where(wide_row == towards, spread_table, 0.0), axis=0, keepdims=True)
    vertex_row = lax.broadcasted_iota(jnp.int32, (LANES, 2 * LANES), 0).astype(jnp.float32) + 1.0
    place = jnp.where(vertex_row == vertex_of, 1.0, 0.0).astype(jnp.bfloat16)
    outgoing = mm(stacked(own), place, NN)
    outgoing = outgoing[:rows] + outgoing[rows:]
    vout[...] = outgoing[:, :LANES]
    own_values = outgoing[:, LANES:]

    columns = own.T
    for k in range(3):
        targets[k] = jnp.broadcast_to(columns[:, fields + k:fields + k + 1], (LANES, LANES))
    row_id = lax.broadcasted_iota(jnp.int32, (rows, 1), 0)
    center = jnp.sum(own * area, axis=1, keepdims=True) / jnp.sum(area)
    center = jnp.where(row_id < fields, center, 0.0)

    pl.semaphore_wait(barrier, n - 1)

    def value_copy(k):
        return pltpu.make_async_remote_copy(
            src_ref=vout, dst_ref=vbuf.at[k], send_sem=vsend.at[k], recv_sem=vrecv.at[k],
            device_id=(lax.rem(my_w + offsets[k], wide), my_b), device_id_type=MESH,
        )

    def term_copy(k):
        return pltpu.make_async_remote_copy(
            src_ref=rout, dst_ref=rbuf.at[k], send_sem=rsend.at[k], recv_sem=rrecv.at[k],
            device_id=(lax.rem(my_w + wide - offsets[k], wide), my_b), device_id_type=MESH,
        )

    def block_copy(step):
        return pltpu.make_async_remote_copy(
            src_ref=blocks.at[0], dst_ref=blocks.at[step], send_sem=bsend.at[step],
            recv_sem=brecv.at[step], device_id=device(step), device_id_type=MESH,
        )

    for k in range(5):
        value_copy(k).start()

    def start_block(step, carry):
        block_copy(step).start()
        return carry

    lax.fori_loop(1, n, start_block, 0)

    corner_rows = []
    for c in range(3):
        corner = corner_ref[0, 0, c:c + 1, :]
        column = jnp.full(corner.shape, -1, jnp.int32)
        for k, offset in enumerate(offsets + (0,)):
            low = lax.rem(my_w + wide - offset, wide) * slot_len
            first = k * slot_len if offset else LANES
            column = jnp.where((corner >= low) & (corner < low + slot_len), corner - low + first, column)
        corner_rows.append(column)
    elements = corner_rows[0].shape[1]
    column = jnp.concatenate(corner_rows, axis=1)
    column_id = lax.broadcasted_iota(jnp.int32, (2 * LANES, 3 * elements), 0)
    pick = jnp.where(column_id == column, 1.0, 0.0).astype(jnp.bfloat16)

    part_lane = lax.broadcasted_iota(jnp.int32, (1, LANES), 1)

    def merged(buffer):
        total = jnp.zeros((rows, LANES), jnp.float32)
        for k in range(5):
            inside = (part_lane >= k * slot_len) & (part_lane < (k + 1) * slot_len)
            total = jnp.where(inside, buffer[k], total)
        return total

    for k in range(5):
        value_copy(k).wait_recv()
    values = jnp.concatenate([merged(vbuf), own_values], axis=1)
    picked = mm(stacked(values), pick, NN)
    picked = picked[:rows] + picked[rows:]
    value_a, value_b, value_c = (picked[:, c * elements:(c + 1) * elements] for c in range(3))
    weight_a, weight_b, weight_c = (weight_ref[0, 0, c:c + 1, :] for c in range(3))
    along_ab = weight_c * (value_a - value_b)
    along_ac = weight_b * (value_a - value_c)
    along_bc = weight_a * (value_b - value_c)
    terms = jnp.concatenate(
        [along_ab + along_ac, along_bc - along_ab, -along_ac - along_bc], axis=1
    )
    returned = mm(stacked(terms), pick, NT)
    returned = returned[:rows] + returned[rows:]
    rout[...] = returned[:, :LANES]
    own_terms = returned[:, LANES:]

    factor_row = row_id < fields

    def add_group(first, acc, sums):
        his, los, weights = [], [], []
        for u in range(GROUP):
            block = blocks[first + u]
            distance = (targets[0] - block[fields:fields + 1]) ** 2
            distance = distance + (targets[1] - block[fields + 1:fields + 2]) ** 2
            distance = distance + (targets[2] - block[fields + 2:fields + 3]) ** 2
            hi, lo = halves(jnp.log(distance + soften))
            mass = (block - center) * jnp.where(factor_row, block[fields + 3:], 1.0)
            sums = sums + mass
            his.append(hi)
            los.append(lo)
            weights.append(stacked(mass))
        weight = jnp.concatenate(weights, axis=1)
        acc = acc + mm(jnp.concatenate(his, axis=1), weight, NT)
        acc = acc + mm(jnp.concatenate(los, axis=1), weight, NT)
        return acc, sums

    for step in range(1, GROUP):
        block_copy(step).wait_recv()
    acc, sums = add_group(
        0, jnp.zeros((LANES, 2 * rows), jnp.float32), jnp.zeros((rows, LANES), jnp.float32)
    )

    for k in range(5):
        term_copy(k).start()

    def one_group(group, carry):
        first = group * GROUP
        for u in range(GROUP):
            block_copy(first + u).wait_recv()
        return add_group(first, *carry)

    acc, sums = lax.fori_loop(1, n // GROUP, one_group, (acc, sums))
    total = acc.T
    total = total[:rows] + total[rows:]
    sums = jnp.sum(sums, axis=1, keepdims=True)
    shift = sums / sums[fields + 3:]
    long_range = -strength * (total - shift * total[fields + 3:])

    for k in range(5):
        term_copy(k).wait_recv()
    back = jnp.concatenate([merged(rbuf), own_terms], axis=1)
    stiffness = mm(stacked(back), place, NT)
    stiffness = stiffness[:rows] + stiffness[rows:]
    result = stiff_coef * stiffness / area + long_range
    out_ref[...] = result[:fields]

    def sent(step, carry):
        block_copy(step).wait_send()
        return carry

    lax.fori_loop(1, n, sent, 0)
    for k in range(5):
        value_copy(k).wait_send()
        term_copy(k).wait_send()


def per_device(position, order_field, cell_area, slot_vertex, send_count, corner_slot, edge_weight):
    fields, local_count = order_field.shape
    wide, blk = lax.axis_size("wide"), lax.axis_size("blk")
    n = wide * blk
    rows = fields + 4
    slot_len = slot_vertex.shape[3]
    vmem = pl.BlockSpec(memory_space=pltpu.VMEM)
    dma = pltpu.SemaphoreType.DMA
    extra = pl.pallas_call(
        functools.partial(kernel, wide, blk, fields, slot_len),
        out_shape=jax.ShapeDtypeStruct((fields, local_count), jnp.float32),
        in_specs=[vmem] * 7,
        out_specs=vmem,
        scratch_shapes=[
            pltpu.VMEM((n, rows, LANES), jnp.float32),
            pltpu.VMEM((rows, LANES), jnp.float32),
            pltpu.VMEM((5, rows, LANES), jnp.float32),
            pltpu.VMEM((rows, LANES), jnp.float32),
            pltpu.VMEM((5, rows, LANES), jnp.float32),
            pltpu.VMEM((3, LANES, LANES), jnp.float32),
            pltpu.VMEM((LANES, 2 * rows), jnp.float32),
            pltpu.VMEM((rows, LANES), jnp.float32),
            dma((n,)), dma((n,)), dma((5,)), dma((5,)), dma((5,)), dma((5,)),
        ],
        compiler_params=pltpu.CompilerParams(collective_id=0, has_side_effects=True),
    )(position, order_field, cell_area.reshape(1, local_count), slot_vertex, send_count,
      corner_slot, edge_weight)
    return order_field**3 - order_field + extra


def solution(mesh):
    placed = (
        P(None, ("wide", "blk")),
        P(None, ("wide", "blk")),
        P(("wide", "blk")),
        P("wide", "blk", None, None),
        P("wide", "blk", None),
        P("wide", "blk", None, None),
        P("wide", "blk", None, None),
    )
    return jax.shard_map(
        per_device, mesh=mesh, in_specs=placed, out_specs=P(None, ("wide", "blk")), check_vma=False
    )
```

```python
import functools

import jax
import jax.numpy as jnp
from jax import lax
from jax.experimental import pallas as pl
from jax.experimental.pallas import tpu as pltpu
from jax.sharding import PartitionSpec as P

stiff_coef = 0.1
LANES = 128
GROUP = 4
MESH = pl.DeviceIdType.MESH
NT = (((1,), (1,)), ((), ()))
NN = (((1,), (0,)), ((), ()))


def halves(x):
    hi = x.astype(jnp.bfloat16)
    lo = (x - hi.astype(jnp.float32)).astype(jnp.bfloat16)
    return hi, lo


def stacked(x):
    return jnp.concatenate(halves(x), axis=0)


def mm(a, b, dims):
    return lax.dot_general(a, b, dims, preferred_element_type=jnp.float32)


def kernel(
    wide, blk, fields, slot_len,
    pos_hbm, order_hbm, area_hbm, slot_hbm, count_hbm, corner_hbm, weight_hbm,
    out_ref,
    pos_ref, order_ref, area_ref, slot_ref, count_ref, corner_ref, weight_ref,
    blocks, vout, vbuf, rout, rbuf, targets,
    isem, bsend, brecv, vsend, vrecv, rsend, rrecv,
):
    n = wide * blk
    my_w, my_b = lax.axis_index("wide"), lax.axis_index("blk")
    me = my_w * blk + my_b
    rows = fields + 4
    soften = 4.0 / (n * LANES)
    strength = float(n * LANES) ** (-0.5)
    offsets = (1, wide - 1, 2, wide - 2, wide // 2)

    def device(step):
        to = lax.rem(me + step, n)
        return (to // blk, lax.rem(to, blk))

    loads = [
        pltpu.make_async_copy(source, held, isem.at[i])
        for i, (source, held) in enumerate((
            (order_hbm, order_ref), (area_hbm, area_ref), (pos_hbm, pos_ref), (slot_hbm, slot_ref),
            (count_hbm, count_ref), (corner_hbm, corner_ref), (weight_hbm, weight_ref),
        ))
    ]
    for load in loads:
        load.start()
    barrier = pltpu.get_barrier_semaphore()

    def greet(step, carry):
        pl.semaphore_signal(barrier, inc=1, device_id=device(step), device_id_type=MESH)
        return carry

    lax.fori_loop(1, n, greet, 0)
    for load in loads:
        load.wait()

    blocks[0, :fields] = order_ref[...]
    blocks[0, fields:fields + 3] = pos_ref[...]
    blocks[0, fields + 3:] = area_ref[...]
    own = jnp.concatenate([order_ref[...], pos_ref[...], area_ref[...]], axis=0)
    area = area_ref[...]

    lane = lax.broadcasted_iota(jnp.int32, (1, 2 * LANES), 1)
    base = jnp.full((1, 2 * LANES), -1, jnp.int32)
    towards = jnp.full((1, 2 * LANES), -1, jnp.int32)
    for k, offset in enumerate(offsets + (0,)):
        first = k * slot_len if offset else LANES
        inside = (lane >= first) & (lane < first + slot_len)
        base = jnp.where(inside, lane - first, base)
        towards = jnp.where(inside, lax.rem(my_w + offset, wide), towards)
    count_lane = lax.broadcasted_iota(jnp.int32, (wide, wide), 1)
    count_row = lax.broadcasted_iota(jnp.int32, (wide, wide), 0)
    counts = count_ref[0].astype(jnp.float32)
    counts = jnp.sum(jnp.where(count_lane == count_row, counts, 0.0), axis=1, keepdims=True)
    slot_id = lax.broadcasted_iota(jnp.int32, (wide, slot_len), 1).astype(jnp.float32)
    table = jnp.where(slot_id < counts, slot_ref[0, 0].astype(jnp.float32) + 1.0, 0.0)
    spread_row = lax.broadcasted_iota(jnp.int32, (slot_len, 2 * LANES), 0)
    spread = jnp.where(spread_row == base, 1.0, 0.0).astype(jnp.bfloat16)
    spread_table = mm(table.astype(jnp.bfloat16), spread, NN)
    wide_row = lax.broadcasted_iota(jnp.int32, (wide, 2 * LANES), 0)
    vertex_of = jnp.sum(jnp.where(wide_row == towards, spread_table, 0.0), axis=0, keepdims=True)
    vertex_row = lax.broadcasted_iota(jnp.int32, (LANES, 2 * LANES), 0).astype(jnp.float32) + 1.0
    place = jnp.where(vertex_row == vertex_of, 1.0, 0.0).astype(jnp.bfloat16)
    outgoing = mm(stacked(own), place, NN)
    outgoing = outgoing[:rows] + outgoing[rows:]
    vout[...] = outgoing[:, :LANES]
    own_values = outgoing[:, LANES:]

    columns = own.T
    for k in range(3):
        targets[k] = jnp.broadcast_to(columns[:, fields + k:fields + k + 1], (LANES, LANES))
    row_id = lax.broadcasted_iota(jnp.int32, (rows, 1), 0)
    center = jnp.sum(own * area, axis=1, keepdims=True) / jnp.sum(area)
    center = jnp.where(row_id < fields, center, 0.0)

    def value_copy(k):
        return pltpu.make_async_remote_copy(
            src_ref=vout, dst_ref=vbuf.at[k], send_sem=vsend.at[k], recv_sem=vrecv.at[k],
            device_id=(lax.rem(my_w + offsets[k], wide), my_b), device_id_type=MESH,
        )

    def term_copy(k):
        return pltpu.make_async_remote_copy(
            src_ref=rout, dst_ref=rbuf.at[k], send_sem=rsend.at[k], recv_sem=rrecv.at[k],
            device_id=(lax.rem(my_w + wide - offsets[k], wide), my_b), device_id_type=MESH,
        )

    def block_copy(step):
        return pltpu.make_async_remote_copy(
            src_ref=blocks.at[0], dst_ref=blocks.at[step], send_sem=bsend.at[step],
            recv_sem=brecv.at[step], device_id=device(step), device_id_type=MESH,
        )

    corner_rows = []
    for c in range(3):
        corner = corner_ref[c]
        column = jnp.full(corner.shape, -1, jnp.int32)
        for k, offset in enumerate(offsets + (0,)):
            low = lax.rem(my_w + wide - offset, wide) * slot_len
            first = k * slot_len if offset else LANES
            column = jnp.where((corner >= low) & (corner < low + slot_len), corner - low + first, column)
        corner_rows.append(column)
    elements = corner_rows[0].shape[1]
    column = jnp.concatenate(corner_rows, axis=1)
    column_id = lax.broadcasted_iota(jnp.int32, (2 * LANES, 3 * elements), 0)
    pick = jnp.where(column_id == column, 1.0, 0.0).astype(jnp.bfloat16)

    pl.semaphore_wait(barrier, n - 1)
    for k in range(5):
        value_copy(k).start()

    def start_block(step, carry):
        block_copy(step).start()
        return carry

    lax.fori_loop(1, n, start_block, 0)

    part_lane = lax.broadcasted_iota(jnp.int32, (1, LANES), 1)

    def merged(buffer):
        total = jnp.zeros((rows, LANES), jnp.float32)
        for k in range(5):
            inside = (part_lane >= k * slot_len) & (part_lane < (k + 1) * slot_len)
            total = jnp.where(inside, buffer[k], total)
        return total

    for k in range(5):
        value_copy(k).wait_recv()
    values = jnp.concatenate([merged(vbuf), own_values], axis=1)
    picked = mm(stacked(values), pick, NN)
    picked = picked[:rows] + picked[rows:]
    value_a, value_b, value_c = (picked[:, c * elements:(c + 1) * elements] for c in range(3))
    weight_a, weight_b, weight_c = (weight_ref[c] for c in range(3))
    along_ab = weight_c * (value_a - value_b)
    along_ac = weight_b * (value_a - value_c)
    along_bc = weight_a * (value_b - value_c)
    terms = jnp.concatenate(
        [along_ab + along_ac, along_bc - along_ab, -along_ac - along_bc], axis=1
    )
    returned = mm(stacked(terms), pick, NT)
    returned = returned[:rows] + returned[rows:]
    rout[...] = returned[:, :LANES]
    own_terms = returned[:, LANES:]

    factor_row = row_id < fields

    def add_group(first, acc, sums):
        his, los, weights = [], [], []
        for u in range(GROUP):
            block = blocks[first + u]
            distance = (targets[0] - block[fields:fields + 1]) ** 2
            distance = distance + (targets[1] - block[fields + 1:fields + 2]) ** 2
            distance = distance + (targets[2] - block[fields + 2:fields + 3]) ** 2
            hi, lo = halves(jnp.log(distance + soften))
            mass = (block - center) * jnp.where(factor_row, block[fields + 3:], 1.0)
            sums = sums + mass
            his.append(hi)
            los.append(lo)
            weights.append(stacked(mass))
        weight = jnp.concatenate(weights, axis=1)
        acc = acc + mm(jnp.concatenate(his, axis=1), weight, NT)
        acc = acc + mm(jnp.concatenate(los, axis=1), weight, NT)
        return acc, sums

    for step in range(1, GROUP):
        block_copy(step).wait_recv()
    acc, sums = add_group(
        0, jnp.zeros((LANES, 2 * rows), jnp.float32), jnp.zeros((rows, LANES), jnp.float32)
    )

    for k in range(5):
        term_copy(k).start()

    def one_group(group, carry):
        first = group * GROUP
        for u in range(GROUP):
            block_copy(first + u).wait_recv()
        return add_group(first, *carry)

    acc, sums = lax.fori_loop(1, n // GROUP, one_group, (acc, sums))
    total = acc.T
    total = total[:rows] + total[rows:]
    sums = jnp.sum(sums, axis=1, keepdims=True)
    shift = sums / sums[fields + 3:]
    long_range = -strength * (total - shift * total[fields + 3:])

    for k in range(5):
        term_copy(k).wait_recv()
    back = jnp.concatenate([merged(rbuf), own_terms], axis=1)
    stiffness = mm(stacked(back), place, NT)
    stiffness = stiffness[:rows] + stiffness[rows:]
    result = stiff_coef * stiffness / area + long_range
    out_ref[...] = result[:fields]

    def sent(step, carry):
        block_copy(step).wait_send()
        return carry

    lax.fori_loop(1, n, sent, 0)
    for k in range(5):
        value_copy(k).wait_send()
        term_copy(k).wait_send()


def per_device(position, order_field, cell_area, slot_vertex, send_count, corner_slot, edge_weight):
    fields, local_count = order_field.shape
    wide, blk = lax.axis_size("wide"), lax.axis_size("blk")
    n = wide * blk
    rows = fields + 4
    slot_len = slot_vertex.shape[3]
    args = (
        position, order_field, cell_area.reshape(1, local_count), slot_vertex, send_count,
        corner_slot.reshape(3, 1, -1), edge_weight.reshape(3, 1, -1),
    )
    vmem = pl.BlockSpec(memory_space=pltpu.VMEM)
    dma = pltpu.SemaphoreType.DMA
    extra = pl.pallas_call(
        functools.partial(kernel, wide, blk, fields, slot_len),
        out_shape=pltpu.VMEM((fields, local_count), jnp.float32),
        in_specs=[pl.BlockSpec(memory_space=pl.ANY)] * 7,
        out_specs=vmem,
        scratch_shapes=[
            *(pltpu.VMEM(x.shape, x.dtype) for x in args),
            pltpu.VMEM((n, rows, LANES), jnp.float32),
            pltpu.VMEM((rows, LANES), jnp.float32),
            pltpu.VMEM((5, rows, LANES), jnp.float32),
            pltpu.VMEM((rows, LANES), jnp.float32),
            pltpu.VMEM((5, rows, LANES), jnp.float32),
            pltpu.VMEM((3, LANES, LANES), jnp.float32),
            dma((7,)), dma((n,)), dma((n,)), dma((5,)), dma((5,)), dma((5,)), dma((5,)),
        ],
        compiler_params=pltpu.CompilerParams(collective_id=0, has_side_effects=True),
    )(*args)
    return order_field**3 - order_field + extra


def solution(mesh):
    placed = (
        P(None, ("wide", "blk")),
        P(None, ("wide", "blk")),
        P(("wide", "blk")),
        P("wide", "blk", None, None),
        P("wide", "blk", None),
        P("wide", "blk", None, None),
        P("wide", "blk", None, None),
    )
    return jax.shard_map(
        per_device, mesh=mesh, in_specs=placed, out_specs=P(None, ("wide", "blk")), check_vma=False
    )
```

```python
import functools

import jax
import jax.numpy as jnp
from jax import lax
from jax.experimental import pallas as pl
from jax.experimental.pallas import tpu as pltpu
from jax.sharding import PartitionSpec as P

stiff_coef = 0.1
LANES = 128
PAD = 32
GROUP = 4
MESH = pl.DeviceIdType.MESH
NT = (((1,), (1,)), ((), ()))
NN = (((1,), (0,)), ((), ()))


def halves(x):
    hi = x.astype(jnp.bfloat16)
    lo = (x - hi.astype(jnp.float32)).astype(jnp.bfloat16)
    return hi, lo


def stacked(x):
    return jnp.concatenate(halves(x), axis=0)


def mm(a, b, dims):
    return lax.dot_general(a, b, dims, preferred_element_type=jnp.float32)


def kernel(
    wide, blk, fields, slot_len,
    pos_hbm, order_hbm, area_hbm, slot_hbm, count_hbm, corner_hbm, weight_hbm,
    out_ref,
    pos_ref, order_ref, area_ref, slot_ref, count_ref, corner_ref, weight_ref,
    blocks, vout, vbuf, kout, kbuf, targets,
    isem, bsend, brecv, vsend, vrecv, ksend, krecv,
):
    n = wide * blk
    my_w, my_b = lax.axis_index("wide"), lax.axis_index("blk")
    me = my_w * blk + my_b
    rows = fields + 4
    soften = 4.0 / (n * LANES)
    strength = float(n * LANES) ** (-0.5)
    offsets = (1, wide - 1, 2, wide - 2, wide // 2)
    around = offsets + (0,)
    spans = sorted({(p - q) % wide for p in around for q in around} - {0})
    total_slots = kbuf.shape[0]

    def device(step):
        to = lax.rem(me + step, n)
        return (to // blk, lax.rem(to, blk))

    loads = [
        pltpu.make_async_copy(source, held, isem.at[i])
        for i, (source, held) in enumerate((
            (order_hbm, order_ref), (area_hbm, area_ref), (pos_hbm, pos_ref), (slot_hbm, slot_ref),
            (count_hbm, count_ref), (corner_hbm, corner_ref), (weight_hbm, weight_ref),
        ))
    ]
    for load in loads:
        load.start()
    barrier = pltpu.get_barrier_semaphore()

    def greet(step, carry):
        pl.semaphore_signal(barrier, inc=1, device_id=device(step), device_id_type=MESH)
        return carry

    lax.fori_loop(1, n, greet, 0)
    for load in loads:
        load.wait()

    blocks[0, :fields] = order_ref[...]
    blocks[0, fields:fields + 3] = pos_ref[...]
    blocks[0, fields + 3:] = area_ref[...]
    own = jnp.concatenate([order_ref[...], pos_ref[...], area_ref[...]], axis=0)
    area = area_ref[...]

    lane = lax.broadcasted_iota(jnp.int32, (1, 2 * LANES), 1)
    base = jnp.full((1, 2 * LANES), -1, jnp.int32)
    towards = jnp.full((1, 2 * LANES), -1, jnp.int32)
    places = [(k * slot_len, offset) for k, offset in enumerate(offsets)]
    places += [(LANES + g * PAD, 0) for g in range(fields // 4)]
    for first, offset in places:
        inside = (lane >= first) & (lane < first + slot_len)
        base = jnp.where(inside, lane - first, base)
        towards = jnp.where(inside, lax.rem(my_w + offset, wide), towards)
    count_lane = lax.broadcasted_iota(jnp.int32, (wide, wide), 1)
    count_row = lax.broadcasted_iota(jnp.int32, (wide, wide), 0)
    counts = count_ref[0].astype(jnp.float32)
    counts = jnp.sum(jnp.where(count_lane == count_row, counts, 0.0), axis=1, keepdims=True)
    slot_id = lax.broadcasted_iota(jnp.int32, (wide, slot_len), 1).astype(jnp.float32)
    table = jnp.where(slot_id < counts, slot_ref[0, 0].astype(jnp.float32) + 1.0, 0.0)
    spread_row = lax.broadcasted_iota(jnp.int32, (slot_len, 2 * LANES), 0)
    spread = jnp.where(spread_row == base, 1.0, 0.0).astype(jnp.bfloat16)
    spread_table = mm(table.astype(jnp.bfloat16), spread, NN)
    wide_row = lax.broadcasted_iota(jnp.int32, (wide, 2 * LANES), 0)
    vertex_of = jnp.sum(jnp.where(wide_row == towards, spread_table, 0.0), axis=0, keepdims=True)
    vertex_row = lax.broadcasted_iota(jnp.int32, (LANES, 2 * LANES), 0).astype(jnp.float32) + 1.0
    place = jnp.where(vertex_row == vertex_of, 1.0, 0.0).astype(jnp.bfloat16)
    outgoing = mm(stacked(own), place, NN)
    outgoing = outgoing[:rows] + outgoing[rows:]
    part_lane = lax.broadcasted_iota(jnp.int32, (1, LANES), 1)
    own_values = outgoing[:, LANES:]
    packed = own_values[:4]
    for g in range(1, fields // 4):
        packed = jnp.where(part_lane >= g * PAD, own_values[4 * g:4 * g + 4], packed)
    vout[:fields] = outgoing[:fields, :LANES]
    vout[fields:] = packed

    columns = own.T
    for k in range(3):
        targets[k] = jnp.broadcast_to(columns[:, fields + k:fields + k + 1], (LANES, LANES))
    row_id = lax.broadcasted_iota(jnp.int32, (rows, 1), 0)
    center = jnp.sum(own * area, axis=1, keepdims=True) / jnp.sum(area)
    center = jnp.where(row_id < fields, center, 0.0)

    def value_copy(k):
        return pltpu.make_async_remote_copy(
            src_ref=vout, dst_ref=vbuf.at[k], send_sem=vsend.at[k], recv_sem=vrecv.at[k],
            device_id=(lax.rem(my_w + k, wide), my_b), device_id_type=MESH,
        )

    def matrix_copy(k):
        part = pl.ds(k * slot_len, slot_len)
        return pltpu.make_async_remote_copy(
            src_ref=kout.at[part], dst_ref=kbuf.at[part], send_sem=ksend.at[k],
            recv_sem=krecv.at[k],
            device_id=(lax.rem(my_w + wide - offsets[k], wide), my_b), device_id_type=MESH,
        )

    def block_copy(step):
        return pltpu.make_async_remote_copy(
            src_ref=blocks.at[0], dst_ref=blocks.at[step], send_sem=bsend.at[step],
            recv_sem=brecv.at[step], device_id=device(step), device_id_type=MESH,
        )

    corner_rows = []
    for c in range(3):
        corner = corner_ref[c]
        column = jnp.full(corner.shape, -1, jnp.int32)
        for k, offset in enumerate(offsets + (0,)):
            low = lax.rem(my_w + wide - offset, wide) * slot_len
            first = k * slot_len if offset else LANES
            column = jnp.where((corner >= low) & (corner < low + slot_len), corner - low + first, column)
        corner_rows.append(column)
    column_id = lax.broadcasted_iota(jnp.int32, (total_slots, 1), 0)
    picks = [jnp.where(column_id == column, 1.0, 0.0) for column in corner_rows]
    signs, heavy, light = [], [], []
    for c in range(3):
        edge = picks[(c + 1) % 3] - picks[(c + 2) % 3]
        hi, lo = (half.astype(jnp.float32) for half in halves(weight_ref[c]))
        signs.append(edge.astype(jnp.bfloat16))
        heavy.append((edge * hi).astype(jnp.bfloat16))
        light.append((edge * lo).astype(jnp.bfloat16))
    signs = jnp.concatenate(signs, axis=1)
    matrix = mm(jnp.concatenate(heavy, axis=1), signs, NT)
    matrix = matrix + mm(jnp.concatenate(light, axis=1), signs, NT)
    kout[...] = matrix
    own_matrix = matrix[LANES:]

    pl.semaphore_wait(barrier, n - 1)
    def start_block(step, carry):
        block_copy(step).start()
        return carry

    lax.fori_loop(1, n, start_block, 0)

    for k in spans:
        value_copy(k).start()
    for k in range(5):
        matrix_copy(k).start()

    factor_row = row_id < fields

    def add_group(first, acc, sums):
        his, los, weights = [], [], []
        for u in range(GROUP):
            block = blocks[first + u]
            distance = (targets[0] - block[fields:fields + 1]) ** 2
            distance = distance + (targets[1] - block[fields + 1:fields + 2]) ** 2
            distance = distance + (targets[2] - block[fields + 2:fields + 3]) ** 2
            hi, lo = halves(jnp.log(distance + soften))
            mass = (block - center) * jnp.where(factor_row, block[fields + 3:], 1.0)
            sums = sums + mass
            his.append(hi)
            los.append(lo)
            weights.append(stacked(mass))
        weight = jnp.concatenate(weights, axis=1)
        acc = acc + mm(jnp.concatenate(his, axis=1), weight, NT)
        acc = acc + mm(jnp.concatenate(los, axis=1), weight, NT)
        return acc, sums

    for step in range(1, GROUP):
        block_copy(step).wait_recv()
    acc, sums = add_group(
        0, jnp.zeros((LANES, 2 * rows), jnp.float32), jnp.zeros((rows, LANES), jnp.float32)
    )

    def one_group(group, carry):
        first = group * GROUP
        for u in range(GROUP):
            block_copy(first + u).wait_recv()
        return add_group(first, *carry)

    acc, sums = lax.fori_loop(1, n // GROUP, one_group, (acc, sums))
    total = acc.T
    total = total[:rows] + total[rows:]
    sums = jnp.sum(sums, axis=1, keepdims=True)
    shift = sums / sums[fields + 3:]
    long_range = -strength * (total - shift * total[fields + 3:])

    for k in spans:
        value_copy(k).wait_recv()
    for k in range(5):
        matrix_copy(k).wait_recv()

    def sent_values(span):
        return vout[...] if span == 0 else vbuf[span]

    gathered = []
    for offset in around:
        total_values = jnp.zeros((rows, LANES), jnp.float32)
        for k in range(5):
            inside = (part_lane >= k * slot_len) & (part_lane < (k + 1) * slot_len)
            total_values = jnp.where(
                inside, sent_values((offsets[k] - offset) % wide), total_values
            )
        packed = sent_values((-offset) % wide)
        parts = [
            (pltpu.roll(packed, LANES - g * PAD, 1) if g else packed)[fields:, :PAD]
            for g in range(fields // 4)
        ]
        parts.append(jnp.zeros((rows - fields, PAD), jnp.float32))
        gathered.append(
            jnp.concatenate([total_values, jnp.concatenate(parts, axis=0)], axis=1)
        )
    gathered = jnp.concatenate(gathered, axis=0)
    high, low = halves(gathered)
    matrix_high, matrix_low = halves(jnp.concatenate([kbuf[:LANES], own_matrix], axis=0))
    product = mm(jnp.concatenate([high, low], axis=0), matrix_high, NT)
    product = product[:6 * rows] + product[6 * rows:] + mm(high, matrix_low, NT)
    slot_lane = lax.broadcasted_iota(jnp.int32, (1, total_slots), 1)
    back = jnp.zeros((rows, total_slots), jnp.float32)
    for k in range(6):
        first = k * slot_len if k < 5 else LANES
        inside = (slot_lane >= first) & (slot_lane < first + slot_len)
        back = jnp.where(inside, product[k * rows:(k + 1) * rows], back)
    place = place[:, :total_slots]
    stiffness = mm(stacked(back), place, NT)
    stiffness = stiffness[:rows] + stiffness[rows:]
    result = stiff_coef * stiffness / area + long_range
    out_ref[...] = result[:fields]

    def sent(step, carry):
        block_copy(step).wait_send()
        return carry

    lax.fori_loop(1, n, sent, 0)
    for k in spans:
        value_copy(k).wait_send()
    for k in range(5):
        matrix_copy(k).wait_send()


def per_device(position, order_field, cell_area, slot_vertex, send_count, corner_slot, edge_weight):
    fields, local_count = order_field.shape
    wide, blk = lax.axis_size("wide"), lax.axis_size("blk")
    n = wide * blk
    rows = fields + 4
    slot_len = slot_vertex.shape[3]
    args = (
        position, order_field, cell_area.reshape(1, local_count), slot_vertex, send_count,
        corner_slot.reshape(3, 1, -1), edge_weight.reshape(3, 1, -1),
    )
    vmem = pl.BlockSpec(memory_space=pltpu.VMEM)
    dma = pltpu.SemaphoreType.DMA
    extra = pl.pallas_call(
        functools.partial(kernel, wide, blk, fields, slot_len),
        out_shape=pltpu.VMEM((fields, local_count), jnp.float32),
        in_specs=[pl.BlockSpec(memory_space=pl.ANY)] * 7,
        out_specs=vmem,
        scratch_shapes=[
            *(pltpu.VMEM(x.shape, x.dtype) for x in args),
            pltpu.VMEM((n, rows, LANES), jnp.float32),
            pltpu.VMEM((rows, LANES), jnp.float32),
            pltpu.VMEM((wide, rows, LANES), jnp.float32),
            pltpu.VMEM((LANES + PAD, LANES + PAD), jnp.float32),
            pltpu.VMEM((LANES + PAD, LANES + PAD), jnp.float32),
            pltpu.VMEM((3, LANES, LANES), jnp.float32),
            dma((7,)), dma((n,)), dma((n,)), dma((wide,)), dma((wide,)), dma((5,)), dma((5,)),
        ],
        compiler_params=pltpu.CompilerParams(collective_id=0, has_side_effects=True),
    )(*args)
    return order_field**3 - order_field + extra


def solution(mesh):
    placed = (
        P(None, ("wide", "blk")),
        P(None, ("wide", "blk")),
        P(("wide", "blk")),
        P("wide", "blk", None, None),
        P("wide", "blk", None),
        P("wide", "blk", None, None),
        P("wide", "blk", None, None),
    )
    return jax.shard_map(
        per_device, mesh=mesh, in_specs=placed, out_specs=P(None, ("wide", "blk")), check_vma=False
    )
```

```python
import functools

import jax
import jax.numpy as jnp
from jax import lax
from jax.experimental import pallas as pl
from jax.experimental.pallas import tpu as pltpu
from jax.sharding import PartitionSpec as P

stiff_coef = 0.1
LANES = 128
PAD = 32
GROUP = 4
MESH = pl.DeviceIdType.MESH
NT = (((1,), (1,)), ((), ()))
NN = (((1,), (0,)), ((), ()))


def halves(x):
    hi = x.astype(jnp.bfloat16)
    lo = (x - hi.astype(jnp.float32)).astype(jnp.bfloat16)
    return hi, lo


def stacked(x):
    return jnp.concatenate(halves(x), axis=0)


def mm(a, b, dims):
    return lax.dot_general(a, b, dims, preferred_element_type=jnp.float32)


def kernel(
    wide, blk, fields, slot_len,
    pos_hbm, order_hbm, area_hbm, slot_hbm, count_hbm, corner_hbm, weight_hbm,
    out_ref,
    pos_ref, order_ref, area_ref, slot_ref, count_ref, corner_ref, weight_ref,
    blocks, vout, vbuf, rout, rbuf, targets,
    isem, bsend, brecv, vsend, vrecv, rsend, rrecv,
):
    n = wide * blk
    my_w, my_b = lax.axis_index("wide"), lax.axis_index("blk")
    me = my_w * blk + my_b
    rows = fields + 4
    soften = 4.0 / (n * LANES)
    strength = float(n * LANES) ** (-0.5)
    offsets = (1, wide - 1, 2, wide - 2, wide // 2)
    total_slots = LANES + PAD

    def device(step):
        to = lax.rem(me + step, n)
        return (to // blk, lax.rem(to, blk))

    loads = [
        pltpu.make_async_copy(source, held, isem.at[i])
        for i, (source, held) in enumerate((
            (order_hbm, order_ref), (area_hbm, area_ref), (pos_hbm, pos_ref), (slot_hbm, slot_ref),
            (count_hbm, count_ref), (corner_hbm, corner_ref), (weight_hbm, weight_ref),
        ))
    ]
    for load in loads:
        load.start()
    barrier = pltpu.get_barrier_semaphore()

    def greet(step, carry):
        pl.semaphore_signal(barrier, inc=1, device_id=device(step), device_id_type=MESH)
        return carry

    lax.fori_loop(1, n, greet, 0)
    for load in loads:
        load.wait()

    blocks[0, :fields] = order_ref[...]
    blocks[0, fields:fields + 3] = pos_ref[...]
    blocks[0, fields + 3:] = area_ref[...]
    own = jnp.concatenate([order_ref[...], pos_ref[...], area_ref[...]], axis=0)
    area = area_ref[...]

    lane = lax.broadcasted_iota(jnp.int32, (1, 2 * LANES), 1)
    base = jnp.full((1, 2 * LANES), -1, jnp.int32)
    towards = jnp.full((1, 2 * LANES), -1, jnp.int32)
    for k, offset in enumerate(offsets + (0,)):
        first = k * slot_len if offset else LANES
        inside = (lane >= first) & (lane < first + slot_len)
        base = jnp.where(inside, lane - first, base)
        towards = jnp.where(inside, lax.rem(my_w + offset, wide), towards)
    count_lane = lax.broadcasted_iota(jnp.int32, (wide, wide), 1)
    count_row = lax.broadcasted_iota(jnp.int32, (wide, wide), 0)
    counts = count_ref[0].astype(jnp.float32)
    counts = jnp.sum(jnp.where(count_lane == count_row, counts, 0.0), axis=1, keepdims=True)
    slot_id = lax.broadcasted_iota(jnp.int32, (wide, slot_len), 1).astype(jnp.float32)
    table = jnp.where(slot_id < counts, slot_ref[0, 0].astype(jnp.float32) + 1.0, 0.0)
    spread_row = lax.broadcasted_iota(jnp.int32, (slot_len, 2 * LANES), 0)
    spread = jnp.where(spread_row == base, 1.0, 0.0).astype(jnp.bfloat16)
    spread_table = mm(table.astype(jnp.bfloat16), spread, NN)
    wide_row = lax.broadcasted_iota(jnp.int32, (wide, 2 * LANES), 0)
    vertex_of = jnp.sum(jnp.where(wide_row == towards, spread_table, 0.0), axis=0, keepdims=True)
    vertex_row = lax.broadcasted_iota(jnp.int32, (LANES, 2 * LANES), 0).astype(jnp.float32) + 1.0
    place = jnp.where(vertex_row == vertex_of, 1.0, 0.0).astype(jnp.bfloat16)
    outgoing = mm(stacked(own), place, NN)
    outgoing = outgoing[:rows] + outgoing[rows:]
    vout[...] = outgoing[:, :LANES]
    own_values = outgoing[:, LANES:]

    def value_copy(k):
        return pltpu.make_async_remote_copy(
            src_ref=vout, dst_ref=vbuf.at[k], send_sem=vsend.at[k], recv_sem=vrecv.at[k],
            device_id=(lax.rem(my_w + offsets[k], wide), my_b), device_id_type=MESH,
        )

    def term_copy(k):
        return pltpu.make_async_remote_copy(
            src_ref=rout, dst_ref=rbuf.at[k], send_sem=rsend.at[k], recv_sem=rrecv.at[k],
            device_id=(lax.rem(my_w + wide - offsets[k], wide), my_b), device_id_type=MESH,
        )

    def block_copy(step):
        return pltpu.make_async_remote_copy(
            src_ref=blocks.at[0], dst_ref=blocks.at[step], send_sem=bsend.at[step],
            recv_sem=brecv.at[step], device_id=device(step), device_id_type=MESH,
        )

    pl.semaphore_wait(barrier, n - 1)
    for k in range(5):
        value_copy(k).start()

    def start_block(step, carry):
        block_copy(step).start()
        return carry

    lax.fori_loop(1, n, start_block, 0)

    corner_rows = []
    for c in range(3):
        corner = corner_ref[c]
        column = jnp.full(corner.shape, -1, jnp.int32)
        for k, offset in enumerate(offsets + (0,)):
            low = lax.rem(my_w + wide - offset, wide) * slot_len
            first = k * slot_len if offset else LANES
            column = jnp.where((corner >= low) & (corner < low + slot_len), corner - low + first, column)
        corner_rows.append(column)
    column_id = lax.broadcasted_iota(jnp.int32, (total_slots, 1), 0)
    picks = [jnp.where(column_id == column, 1.0, 0.0) for column in corner_rows]
    signs, heavy, light = [], [], []
    for c in range(3):
        edge = picks[(c + 1) % 3] - picks[(c + 2) % 3]
        hi, lo = (half.astype(jnp.float32) for half in halves(weight_ref[c]))
        signs.append(edge.astype(jnp.bfloat16))
        heavy.append((edge * hi).astype(jnp.bfloat16))
        light.append((edge * lo).astype(jnp.bfloat16))
    signs = jnp.concatenate(signs, axis=1)
    matrix = mm(jnp.concatenate(heavy, axis=1), signs, NT)
    matrix = matrix + mm(jnp.concatenate(light, axis=1), signs, NT)
    matrix_high, matrix_low = halves(matrix)

    columns = own.T
    for k in range(3):
        targets[k] = jnp.broadcast_to(columns[:, fields + k:fields + k + 1], (LANES, LANES))
    row_id = lax.broadcasted_iota(jnp.int32, (rows, 1), 0)
    center = jnp.sum(own * area, axis=1, keepdims=True) / jnp.sum(area)
    center = jnp.where(row_id < fields, center, 0.0)

    part_lane = lax.broadcasted_iota(jnp.int32, (1, LANES), 1)

    def merged(buffer):
        total = jnp.zeros((rows, LANES), jnp.float32)
        for k in range(5):
            inside = (part_lane >= k * slot_len) & (part_lane < (k + 1) * slot_len)
            total = jnp.where(inside, buffer[k], total)
        return total

    for k in range(5):
        value_copy(k).wait_recv()
    values = jnp.concatenate([merged(vbuf), own_values[:, :PAD]], axis=1)
    high, low = halves(values)
    returned = mm(jnp.concatenate([high, low], axis=0), matrix_high, NN)
    returned = returned[:rows] + returned[rows:] + mm(high, matrix_low, NN)
    rout[...] = returned[:, :LANES]
    own_terms = returned[:, LANES:]

    factor_row = row_id < fields

    def add_group(first, acc, sums):
        his, los, weights = [], [], []
        for u in range(GROUP):
            block = blocks[first + u]
            distance = (targets[0] - block[fields:fields + 1]) ** 2
            distance = distance + (targets[1] - block[fields + 1:fields + 2]) ** 2
            distance = distance + (targets[2] - block[fields + 2:fields + 3]) ** 2
            hi, lo = halves(jnp.log(distance + soften))
            mass = (block - center) * jnp.where(factor_row, block[fields + 3:], 1.0)
            sums = sums + mass
            his.append(hi)
            los.append(lo)
            weights.append(stacked(mass))
        weight = jnp.concatenate(weights, axis=1)
        acc = acc + mm(jnp.concatenate(his, axis=1), weight, NT)
        acc = acc + mm(jnp.concatenate(los, axis=1), weight, NT)
        return acc, sums

    for step in range(1, GROUP):
        block_copy(step).wait_recv()
    acc, sums = add_group(
        0, jnp.zeros((LANES, 2 * rows), jnp.float32), jnp.zeros((rows, LANES), jnp.float32)
    )

    for k in range(5):
        term_copy(k).start()

    def one_group(group, carry):
        first = group * GROUP
        for u in range(GROUP):
            block_copy(first + u).wait_recv()
        return add_group(first, *carry)

    acc, sums = lax.fori_loop(1, n // GROUP, one_group, (acc, sums))
    total = acc.T
    total = total[:rows] + total[rows:]
    sums = jnp.sum(sums, axis=1, keepdims=True)
    shift = sums / sums[fields + 3:]
    long_range = -strength * (total - shift * total[fields + 3:])

    def sent(step, carry):
        block_copy(step).wait_send()
        return carry

    lax.fori_loop(1, n, sent, 0)
    for k in range(5):
        term_copy(k).wait_recv()
    back = jnp.concatenate([merged(rbuf), own_terms], axis=1)
    stiffness = mm(stacked(back), place[:, :total_slots], NT)
    stiffness = stiffness[:rows] + stiffness[rows:]
    result = stiff_coef * stiffness / area + long_range
    out_ref[...] = result[:fields]

    for k in range(5):
        value_copy(k).wait_send()
        term_copy(k).wait_send()


def per_device(position, order_field, cell_area, slot_vertex, send_count, corner_slot, edge_weight):
    fields, local_count = order_field.shape
    wide, blk = lax.axis_size("wide"), lax.axis_size("blk")
    n = wide * blk
    rows = fields + 4
    slot_len = slot_vertex.shape[3]
    args = (
        position, order_field, cell_area.reshape(1, local_count), slot_vertex, send_count,
        corner_slot.reshape(3, 1, -1), edge_weight.reshape(3, 1, -1),
    )
    vmem = pl.BlockSpec(memory_space=pltpu.VMEM)
    dma = pltpu.SemaphoreType.DMA
    extra = pl.pallas_call(
        functools.partial(kernel, wide, blk, fields, slot_len),
        out_shape=pltpu.VMEM((fields, local_count), jnp.float32),
        in_specs=[pl.BlockSpec(memory_space=pl.ANY)] * 7,
        out_specs=vmem,
        scratch_shapes=[
            *(pltpu.VMEM(x.shape, x.dtype) for x in args),
            pltpu.VMEM((n, rows, LANES), jnp.float32),
            pltpu.VMEM((rows, LANES), jnp.float32),
            pltpu.VMEM((5, rows, LANES), jnp.float32),
            pltpu.VMEM((rows, LANES), jnp.float32),
            pltpu.VMEM((5, rows, LANES), jnp.float32),
            pltpu.VMEM((3, LANES, LANES), jnp.float32),
            dma((7,)), dma((n,)), dma((n,)), dma((5,)), dma((5,)), dma((5,)), dma((5,)),
        ],
        compiler_params=pltpu.CompilerParams(collective_id=0, has_side_effects=True),
    )(*args)
    return order_field**3 - order_field + extra


def solution(mesh):
    placed = (
        P(None, ("wide", "blk")),
        P(None, ("wide", "blk")),
        P(("wide", "blk")),
        P("wide", "blk", None, None),
        P("wide", "blk", None),
        P("wide", "blk", None, None),
        P("wide", "blk", None, None),
    )
    return jax.shard_map(
        per_device, mesh=mesh, in_specs=placed, out_specs=P(None, ("wide", "blk")), check_vma=False
    )
```
